32 devices in a mesh: dp: 4 (over y, x), fsdp: 8 (over z, core).
Axes of the slice: x: 2, y: 2, z: 4, core: 2. Of those that a mesh axis runs over, the one named last changes fastest.
Arguments:
- inputs: bfloat16 [512, 16384], P('dp', 'fsdp'), may hold values from -140 to 140
- norm_gain_vector: bfloat16 [16384], P('fsdp'), may hold values from 0.5 to 1.5
- weight: bfloat16 [16384, 16384], P(None, 'fsdp'), may hold values from -0.046875 to 0.046875
- down_adapters: bfloat16 [16384, 16, 32], P('fsdp'), may hold values from -0.046875 to 0.046875
- up_adapters: bfloat16 [16, 32, 16384], P(None, None, 'fsdp'), may hold values from -1 to 1
- tenant: int32 [512], P('dp'), may hold values from 0 to 15
- tenant_slot_index: int32 [16], replicated, may hold values from 0 to 31, as said below
- live_row_count: int32 [4], P('dp'), may hold values from 1 to 128, 320 in all
- cotangent: bfloat16 [512, 16384], P('dp', 'fsdp'), may hold values from -6 to 6
- down_row_factor: float32 [32, 16384], P('dp', 'fsdp'), may hold values from 300 to 30000
- down_column_factor: float32 [32, 32], P('dp'), may hold values from 300 to 30000
- up_row_factor: float32 [32, 32], P('dp'), may hold values from 0.5 to 50
- up_column_factor: float32 [32, 16384], P('dp', 'fsdp'), may hold values from 0.5 to 50
Outputs:
- projected: bfloat16 [512, 16384], P('dp', 'fsdp')
- normed_gradient_transposed: bfloat16 [16384, 512], P('fsdp', 'dp')
- update_a: float32 [32, 16384, 32], P('dp', 'fsdp')
- update_b: float32 [32, 32, 16384], P('dp', None, 'fsdp')
- row_a_new: float32 [32, 16384], P('dp', 'fsdp')
- col_a_new: float32 [32, 32], P('dp')
- row_b_new: float32 [32, 32], P('dp')
- col_b_new: float32 [32, 16384], P('dp', 'fsdp')
The draws below stay inside these ranges and needn't reach their ends.
Inputs may be any that keep to these rules, and one draw needn't show every extreme that they name: Distinct slots; tenant t's optimizer state is in slot tenant_slot_index[t], owned by data group tenant_slot_index[t] // 8; every group owns at most 8 tenants and some group owns exactly 8. The first live_row_count[g] rows of data group g are live; some group has all 128 live; the counts sum to 320.
All inputs are finite; a program needn't handle non-finite values.
Results may differ from the reference program's by a relative error of at most 0.0095.
Values may be sent and summed in bfloat16 or wider, within the bound.
A program may use at most 192 MiB of HBM per device.

```python
import math
import jax
import jax.numpy as jnp
import numpy as np
from jax import lax

MODEL_WIDTH = 16384
ADAPTER_RANK = 32
TENANT_COUNT = 16
CAP = 8
ROWS = 128
ROWS_ALL = 512
SLOTS = 32
N_DP = 4


def draw_inputs(key, part):
    key_base, key_cols, key_rows = jax.random.split(jax.random.fold_in(key, 11), 3)
    position = jnp.arange(MODEL_WIDTH, dtype=jnp.float32) / MODEL_WIDTH
    columns = jnp.exp(jnp.log(3.0) * position) * jnp.exp(jax.random.uniform(key_cols, (MODEL_WIDTH,), jnp.float32, 0.0, 1.2))
    rowscale = jnp.exp(jax.random.uniform(key_rows, (ROWS_ALL, 1), jnp.float32, 0.0, jnp.log(10.0)))
    frozen_output = jnp.clip(jax.random.normal(key_base, (ROWS_ALL, MODEL_WIDTH), jnp.float32), -4.0, 4.0)
    return (frozen_output * columns[None, :] * rowscale / 3.0).astype(jnp.bfloat16)


def draw_tenant_slot_index(key, part):
    key_full, key_order, key_other = jax.random.split(jax.random.fold_in(key, 23), 3)
    full = jax.random.randint(key_full, (), 0, N_DP)
    order = jax.random.permutation(key_order, TENANT_COUNT)
    others = jax.random.permutation(key_other, (N_DP - 1) * CAP)
    group = others // CAP
    group = group + (group >= full).astype(jnp.int32)
    other_slots = (group * CAP + others % CAP).astype(jnp.int32)
    filler = jnp.concatenate([jnp.zeros((CAP,), jnp.int32), other_slots[:TENANT_COUNT - CAP]])
    ranked = jnp.arange(TENANT_COUNT, dtype=jnp.int32)
    slot_by_rank = jnp.where(ranked < CAP, full * CAP + ranked, filler).astype(jnp.int32)
    return jnp.zeros((TENANT_COUNT,), jnp.int32).at[order].set(slot_by_rank)


def set_ends(result, stream_key, low, largest):
    longest = result.shape.index(max(result.shape))
    spots = []
    for shift in (0, 1):
        where = [jax.random.randint(jax.random.fold_in(stream_key, axis), (), 0, length) for axis, length in enumerate(result.shape)]
        where[longest] = (where[longest] + shift) % result.shape[longest]
        spots.append(tuple(where))
    return result.at[spots[0]].set(low).at[spots[1]].set(largest)


def block_scale(stream_key, dims, cuts, smallest, largest):
    factor_of, own = 1.0, jax.random.fold_in(stream_key, 6)
    for axis_at, blocks in cuts:
        steps = jnp.exp(jax.random.uniform(jax.random.fold_in(own, axis_at), (blocks,), jnp.float32, smallest / len(cuts), largest / len(cuts)))
        factor_of = factor_of * jnp.repeat(steps, dims[axis_at] // blocks).reshape([-1 if axis == axis_at else 1 for axis in range(len(dims))])
    return factor_of


def cumulative_ranks(count, lean):
    loads = [(1 << 20) // math.isqrt(rank ** lean) + 1 for rank in range(1, count + 1)]
    width = 1 + sum(loads) // (1 << 30)
    return np.cumsum(np.array([max(1, weight // width) for weight in loads]))


def skewed_ids(stream_key, dims, number_of, lean):
    table = cumulative_ranks(number_of, lean)
    ticket = jax.random.randint(jax.random.fold_in(stream_key, 1), dims, 0, int(table[number_of - 1]))
    rank = jnp.searchsorted(jnp.asarray(table, jnp.int32), ticket, side="right")
    return jax.random.permutation(jax.random.fold_in(stream_key, 2), number_of)[rank].astype(jnp.int32)


def split_up(number_of, total, most, lean):
    loads = [(1 << 20) // math.isqrt(standing ** lean) + 1 for standing in range(2, number_of + 1)]
    spare, counts = total - most - (number_of - 1), [1] * (number_of - 1)
    while spare > 0:
        candidates = [i for i in range(number_of - 1) if counts[i] < most]
        pool, budget = sum([loads[i] for i in candidates]), spare
        for i in candidates:
            addition = min(most - counts[i], max(1, budget * loads[i] // pool), spare)
            counts[i] = counts[i] + addition
            spare = spare - addition
    return np.array([most] + counts)


def uneven(rng, number_of, total, bound, slope):
    if number_of == 2:
        one = jax.random.randint(rng, (), max(1, total - bound), min(bound, total - 1) + 1)
        return jnp.stack([one, total - one])
    lengths = jnp.asarray(split_up(number_of, total, bound, slope), jnp.int32)
    couples = (number_of - 1) // 2
    giver, taker = lengths[1:1 + 2 * couples:2], lengths[2:2 + 2 * couples:2]
    margin = jnp.minimum(giver - 1, bound - taker)
    shifted = jax.random.randint(jax.random.fold_in(rng, 1), (couples,), 0, 1 << 20) % (margin + 1)
    lengths = lengths.at[1:1 + 2 * couples:2].set(giver - shifted).at[2:2 + 2 * couples:2].set(taker + shifted)
    return lengths[jax.random.permutation(jax.random.fold_in(rng, 2), number_of)]


def gaussian(stream_key, shape, deviation, most, shards=(), kind=jnp.bfloat16):
    values = deviation * jax.random.normal(stream_key, shape, jnp.float32)
    if shards:
        values = values * block_scale(stream_key, shape, shards, -0.22, 0.18)
    return jnp.clip(values, -most, most).astype(kind)


def setup_inputs(seed: int = 0) -> dict:
    splits = jax.random.split(jax.random.key(seed), 14)
    inputs = draw_inputs(jax.random.fold_in(splits[13], 71), 0)
    norm_gain_vector = jnp.clip(1.0 + 0.1 * jax.random.normal(splits[1], (MODEL_WIDTH,), jnp.float32), 0.5, 1.5).astype(jnp.bfloat16)
    weight = gaussian(splits[2], (MODEL_WIDTH, MODEL_WIDTH), MODEL_WIDTH ** -0.5, 0.046875, ((1, 8),))
    down_adapters = gaussian(splits[3], (MODEL_WIDTH, TENANT_COUNT, ADAPTER_RANK), MODEL_WIDTH ** -0.5, 0.046875, ((0, 8),))
    up_adapters = gaussian(splits[4], (TENANT_COUNT, ADAPTER_RANK, MODEL_WIDTH), ADAPTER_RANK ** -0.5, 1.0, ((2, 8),))
    tenant = set_ends(skewed_ids(splits[5], (ROWS_ALL,), TENANT_COUNT, 2), jax.random.fold_in(splits[5], 3), 0, TENANT_COUNT - 1).astype(jnp.int32)
    tenant_slot_index = draw_tenant_slot_index(jax.random.fold_in(splits[13], 71), 0)
    live_row_count = uneven(splits[7], N_DP, (N_DP + 1) * ROWS // 2, ROWS, 0).astype(jnp.int32)
    cotangent = gaussian(splits[8], (ROWS_ALL, MODEL_WIDTH), 1.0, 6.0, ((0, 4), (1, 8)))
    down_row_factor = jnp.clip(jnp.exp(math.log(30000.0) - 4.6051702 * jax.random.uniform(splits[9], (SLOTS, MODEL_WIDTH), jnp.float32) ** block_scale(splits[9], (SLOTS, MODEL_WIDTH), ((0, 4), (1, 8)), -0.2, 0.2)), 300.0, 30000.0)
    down_column_factor = jnp.clip(jnp.exp(math.log(30000.0) - 4.6051702 * jax.random.uniform(splits[10], (SLOTS, ADAPTER_RANK), jnp.float32) ** block_scale(splits[10], (SLOTS, ADAPTER_RANK), ((0, 4),), -0.2, 0.2)), 300.0, 30000.0)
    up_row_factor = jnp.clip(jnp.exp(math.log(50.0) - 4.6051702 * jax.random.uniform(splits[11], (SLOTS, ADAPTER_RANK), jnp.float32) ** block_scale(splits[11], (SLOTS, ADAPTER_RANK), ((0, 4),), -0.2, 0.2)), 0.5, 50.0)
    up_column_factor = jnp.clip(jnp.exp(math.log(50.0) - 4.6051702 * jax.random.uniform(splits[12], (SLOTS, MODEL_WIDTH), jnp.float32) ** block_scale(splits[12], (SLOTS, MODEL_WIDTH), ((0, 4), (1, 8)), -0.2, 0.2)), 0.5, 50.0)
    return dict(inputs=inputs, norm_gain_vector=norm_gain_vector, weight=weight, down_adapters=down_adapters, up_adapters=up_adapters, tenant=tenant, tenant_slot_index=tenant_slot_index, live_row_count=live_row_count, cotangent=cotangent, down_row_factor=down_row_factor, down_column_factor=down_column_factor, up_row_factor=up_row_factor, up_column_factor=up_column_factor)


ADAPTER_SCALE = 0.5
BETA_TWO = 0.9
SQ_EPS = 1e-30
RMS_EPS = 1e-05

def reference(inputs, norm_gain_vector, weight, down_adapters, up_adapters, tenant, tenant_slot_index, live_row_count, cotangent, down_row_factor, down_column_factor, up_row_factor, up_column_factor):
    highest_precision = lax.Precision.HIGHEST
    xf = inputs.astype(jnp.float32)
    power = lax.optimization_barrier(jnp.sum(xf * xf, axis=1, keepdims=True))
    scale = lax.rsqrt(power / MODEL_WIDTH + RMS_EPS)
    normalized_input = (xf * scale * norm_gain_vector.astype(jnp.float32)).astype(jnp.bfloat16)
    pick = tenant[:, None] == jnp.arange(TENANT_COUNT, dtype=jnp.int32)[None, :]
    pick_b = pick.astype(jnp.bfloat16)
    pick_f = pick.astype(jnp.float32)
    down_flattened = down_adapters.reshape(MODEL_WIDTH, TENANT_COUNT * ADAPTER_RANK)
    up_flattened = up_adapters.reshape(TENANT_COUNT * ADAPTER_RANK, MODEL_WIDTH)
    inner_all = jnp.dot(normalized_input, down_flattened, preferred_element_type=jnp.float32)
    inner = lax.optimization_barrier(jnp.sum(inner_all.reshape(ROWS_ALL, TENANT_COUNT, ADAPTER_RANK) * pick_f[:, :, None], axis=1))
    spread_rows = (inner.astype(jnp.bfloat16)[:, None, :] * pick_b[:, :, None]).reshape(ROWS_ALL, TENANT_COUNT * ADAPTER_RANK)
    frozen_output = jnp.dot(normalized_input, weight, preferred_element_type=jnp.float32)
    adapted_output = jnp.dot(spread_rows, up_flattened, preferred_element_type=jnp.float32)
    projected = (frozen_output + ADAPTER_SCALE * adapted_output).astype(jnp.bfloat16)
    index = jnp.arange(ROWS_ALL, dtype=jnp.int32)
    live = index % ROWS < live_row_count[index // ROWS]
    output_gradient = jnp.where(live[:, None], cotangent, jnp.zeros_like(cotangent))
    back_all = jnp.dot(output_gradient, up_flattened.T, preferred_element_type=jnp.float32)
    back = lax.optimization_barrier(jnp.sum(back_all.reshape(ROWS_ALL, TENANT_COUNT, ADAPTER_RANK) * pick_f[:, :, None], axis=1))
    backward_spread_rows = (back.astype(jnp.bfloat16)[:, None, :] * pick_b[:, :, None]).reshape(ROWS_ALL, TENANT_COUNT * ADAPTER_RANK)
    frozen_input_gradient = jnp.dot(weight, output_gradient.T, preferred_element_type=jnp.float32)
    adapter_input_gradient = jnp.dot(down_flattened, backward_spread_rows.T, preferred_element_type=jnp.float32)
    normed_gradient_transposed = (frozen_input_gradient + ADAPTER_SCALE * adapter_input_gradient).astype(jnp.bfloat16)
    down_gradient = (ADAPTER_SCALE * jnp.dot(normalized_input.T, backward_spread_rows, preferred_element_type=jnp.float32)).reshape(MODEL_WIDTH, TENANT_COUNT, ADAPTER_RANK)
    up_gradient = (ADAPTER_SCALE * jnp.dot(spread_rows.T, output_gradient, preferred_element_type=jnp.float32)).reshape(TENANT_COUNT, ADAPTER_RANK, MODEL_WIDTH)
    owner_routing = (tenant_slot_index[None, :] == jnp.arange(SLOTS, dtype=jnp.int32)[:, None]).astype(jnp.float32)
    ga = jnp.einsum('st,dtr->sdr', owner_routing, down_gradient, precision=highest_precision)
    gb = jnp.einsum('st,trd->srd', owner_routing, up_gradient, precision=highest_precision)
    sq_a = ga * ga + SQ_EPS
    sq_b = gb * gb + SQ_EPS
    row_a_new = BETA_TWO * down_row_factor + (1.0 - BETA_TWO) * (lax.optimization_barrier(jnp.sum(sq_a, axis=2)) / ADAPTER_RANK)
    col_a_new = BETA_TWO * down_column_factor + (1.0 - BETA_TWO) * (lax.optimization_barrier(jnp.sum(sq_a, axis=1)) / MODEL_WIDTH)
    row_b_new = BETA_TWO * up_row_factor + (1.0 - BETA_TWO) * (lax.optimization_barrier(jnp.sum(sq_b, axis=2)) / MODEL_WIDTH)
    col_b_new = BETA_TWO * up_column_factor + (1.0 - BETA_TWO) * (lax.optimization_barrier(jnp.sum(sq_b, axis=1)) / ADAPTER_RANK)
    mean_a = lax.optimization_barrier(jnp.sum(row_a_new, axis=1)) / MODEL_WIDTH
    mean_b = lax.optimization_barrier(jnp.sum(row_b_new, axis=1)) / ADAPTER_RANK
    update_a = ga * lax.rsqrt(row_a_new[:, :, None] * col_a_new[:, None, :] / mean_a[:, None, None])
    update_b = gb * lax.rsqrt(row_b_new[:, :, None] * col_b_new[:, None, :] / mean_b[:, None, None])
    return (projected, normed_gradient_transposed, update_a, update_b, row_a_new, col_a_new, row_b_new, col_b_new)
```

```python
import jax
import jax.numpy as jnp
from jax import lax
from jax.sharding import PartitionSpec as P

ADAPTER_SCALE = 0.5
BETA_TWO = 0.9
SQ_EPS = 1e-30
RMS_EPS = 1e-05

CONTRACT_LAST = (((1,), (1,)), ((), ()))


def on_device(
    inputs,
    norm_gain_vector,
    weight,
    down_adapters,
    up_adapters,
    tenant,
    tenant_slot_index,
    live_row_count,
    cotangent,
    down_row_factor,
    down_column_factor,
    up_row_factor,
    up_column_factor,
):
    rows, local = inputs.shape
    width = weight.shape[0]
    tenants, rank = down_adapters.shape[1:]
    owned = down_row_factor.shape[0]
    f32, bf16 = jnp.float32, jnp.bfloat16
    xf = inputs.astype(f32)
    gained = (xf * norm_gain_vector.astype(f32)).astype(bf16)
    live = lax.iota(jnp.int32, rows) < live_row_count[0]
    grad_out = jnp.where(live[:, None], cotangent, jnp.zeros_like(cotangent))
    gained_all = lax.all_gather(gained, "fsdp", axis=1, tiled=True)
    grad_in = lax.psum_scatter(
        lax.dot_general(weight, grad_out, CONTRACT_LAST, preferred_element_type=f32).astype(bf16),
        "fsdp",
        scatter_dimension=0,
        tiled=True,
    )
    pick = tenant[:, None] == lax.iota(jnp.int32, tenants)[None, :]
    pick_f = pick.astype(f32)
    down = down_adapters.reshape(local, tenants * rank)
    up = up_adapters.reshape(tenants * rank, local)
    inner_all = jnp.dot(gained, down, preferred_element_type=f32)
    back_all = lax.dot_general(grad_out, up, CONTRACT_LAST, preferred_element_type=f32)

    def own(z):
        return jnp.sum(z.reshape(rows, tenants, rank) * pick_f[:, :, None], axis=1)

    packed = lax.psum(
        jnp.concatenate(
            [own(inner_all), own(back_all), jnp.sum(xf * xf, axis=1, keepdims=True)], axis=1
        ),
        "fsdp",
    )
    scale = lax.rsqrt(packed[:, 2 * rank :] / width + RMS_EPS)
    inner = packed[:, :rank] * scale
    back = packed[:, rank : 2 * rank]

    def spread(z, mask):
        return (z.astype(bf16)[:, None, :] * mask.astype(bf16)[:, :, None]).reshape(z.shape[0], -1)

    adapted = jnp.dot(spread(inner, pick), up, preferred_element_type=f32)
    frozen = jnp.dot(gained_all, weight, preferred_element_type=f32)
    projected = (frozen * scale + ADAPTER_SCALE * adapted).astype(bf16)
    adapter_in = lax.dot_general(down, spread(back, pick), CONTRACT_LAST, preferred_element_type=f32)
    grad_t = (grad_in.astype(f32) + ADAPTER_SCALE * adapter_in).astype(bf16)

    slot = jnp.sum(jnp.where(pick, tenant_slot_index[None, :], 0), axis=1)
    small = jnp.concatenate([inner, back * scale, slot.astype(f32)[:, None]], axis=1)
    small_all = lax.all_gather(small, "dp", axis=0, tiled=True)
    rows_all = lax.all_gather(gained, "dp", axis=0, tiled=True)
    grad_all = lax.all_gather(grad_out, "dp", axis=0, tiled=True)
    mine = lax.iota(jnp.int32, owned) + lax.axis_index("dp") * owned
    route = small_all[:, 2 * rank :].astype(jnp.int32) == mine[None, :]
    first = (((0,), (0,)), ((), ()))
    ga = ADAPTER_SCALE * lax.dot_general(
        spread(small_all[:, rank : 2 * rank], route), rows_all, first, preferred_element_type=f32
    ).reshape(owned, rank, local)
    gb = ADAPTER_SCALE * lax.dot_general(
        spread(small_all[:, :rank], route), grad_all, first, preferred_element_type=f32
    ).reshape(owned, rank, local)
    sq_a = ga * ga + SQ_EPS
    sq_b = gb * gb + SQ_EPS
    row_a_new = BETA_TWO * down_row_factor + (1.0 - BETA_TWO) * (jnp.sum(sq_a, axis=1) / rank)
    col_b_new = BETA_TWO * up_column_factor + (1.0 - BETA_TWO) * (jnp.sum(sq_b, axis=1) / rank)
    sums = lax.psum(
        jnp.concatenate(
            [jnp.sum(sq_a, axis=2), jnp.sum(sq_b, axis=2), jnp.sum(row_a_new, axis=1)[:, None]],
            axis=1,
        ),
        "fsdp",
    )
    col_a_new = BETA_TWO * down_column_factor + (1.0 - BETA_TWO) * (sums[:, :rank] / width)
    row_b_new = BETA_TWO * up_row_factor + (1.0 - BETA_TWO) * (sums[:, rank : 2 * rank] / width)
    mean_a = sums[:, 2 * rank] / width
    mean_b = jnp.sum(row_b_new, axis=1) / rank
    update_a = ga * lax.rsqrt(row_a_new[:, None, :] * col_a_new[:, :, None] / mean_a[:, None, None])
    update_b = gb * lax.rsqrt(row_b_new[:, :, None] * col_b_new[:, None, :] / mean_b[:, None, None])
    return (
        projected,
        grad_t,
        jnp.swapaxes(update_a, 1, 2),
        update_b,
        row_a_new,
        col_a_new,
        row_b_new,
        col_b_new,
    )


def solution(mesh):
    return jax.shard_map(
        on_device,
        mesh=mesh,
        in_specs=(
            P("dp", "fsdp"),
            P("fsdp"),
            P(None, "fsdp"),
            P("fsdp", None, None),
            P(None, None, "fsdp"),
            P("dp"),
            P(),
            P("dp"),
            P("dp", "fsdp"),
            P("dp", "fsdp"),
            P("dp", None),
            P("dp", None),
            P("dp", "fsdp"),
        ),
        out_specs=(
            P("dp", "fsdp"),
            P("fsdp", "dp"),
            P("dp", "fsdp", None),
            P("dp", None, "fsdp"),
            P("dp", "fsdp"),
            P("dp", None),
            P("dp", None),
            P("dp", "fsdp"),
        ),
        check_vma=False,
    )
```

```python
import functools

import jax
import jax.numpy as jnp
from jax import lax
from jax.experimental import pallas as pl
from jax.experimental.pallas import tpu as pltpu
from jax.sharding import PartitionSpec as P

ADAPTER_SCALE = 0.5
BETA_TWO = 0.9
SQ_EPS = 1e-30
RMS_EPS = 1e-05
BUFFERS = 3
NT = (((1,), (1,)), ((), ()))
TN = (((0,), (0,)), ((), ()))
F32, BF16 = jnp.float32, jnp.bfloat16
MESH = pl.DeviceIdType.MESH


def xor(a, b, count):
    out, bit = 0, 1
    while bit < count:
        out = out + ((a // bit + b // bit) % 2) * bit
        bit *= 2
    return out


def kernel(
    ndp, n, rank, tenants, owned, width,
    gained, grad, meta, down, up, weight,
    projected, grad_t, ga, gb, sum_a, sum_b, stats,
    wbuf, ag, dpx, dpg, acc, part, psend, prx, csend, uprx, dnrx,
    pk, pkrx, sm, smrx, st, strx, spread_a, spread_b, lanes, scale_col,
    wsem, ag_s, ag_sp, ag_r, dp_s, dp_r, pp_s, pp_r, ch_s, up_r, dn_r, pk_s, pk_r, st_s, st_r,
):
    rows, local = gained.shape
    tile = wbuf.shape[1]
    tpb = local // tile
    nq = n // 2
    count = 2 * nq * tpb
    d = lax.axis_index("dp")
    f = lax.axis_index("fsdp")
    q, c = f // 2, f % 2
    mate = 2 * q + 1 - c

    def remote(src, dst, ssem, rsem, **where):
        return pltpu.make_async_remote_copy(
            src_ref=src, dst_ref=dst, send_sem=ssem, recv_sem=rsem,
            device_id=where, device_id_type=MESH,
        )

    def start_row(i):
        i2 = i % count
        back = i // count == 0
        s, r = i2 // (2 * tpb), i2 % (2 * tpb)
        half = r // tpb
        t = xor(q, jnp.where(back, nq - 1 - s, s), nq)
        core = jnp.where(back, (1 - c) * (1 - half) + c * half, c * (1 - half) + (1 - c) * half)
        return (2 * t + core) * local + (r % tpb) * tile

    def load(i):
        return pltpu.make_async_copy(
            weight.at[pl.ds(pl.multiple_of(start_row(i), tile), tile), :],
            wbuf.at[i % BUFFERS], wsem.at[i % BUFFERS],
        )

    for i in range(BUFFERS):
        load(jnp.int32(i)).start()

    barrier = pltpu.get_barrier_semaphore()
    for k in range(1, n):
        pl.semaphore_signal(barrier, inc=1, device_id={"fsdp": (f + k) % n}, device_id_type=MESH)
    for k in range(1, ndp):
        pl.semaphore_signal(barrier, inc=1, device_id={"dp": (d + k) % ndp}, device_id_type=MESH)
    pl.semaphore_wait(barrier, n - 1 + ndp - 1)

    def ag_up(slot, src):
        return remote(src, ag.at[slot], ag_s.at[slot, 0], ag_r.at[slot], fsdp=(f + 2) % n)

    def ag_down(slot, src):
        return remote(src, ag.at[slot], ag_s.at[slot, 1], ag_r.at[slot], fsdp=(f + n - 2) % n)

    def ag_mate(slot, src):
        return remote(src, ag.at[slot], ag_sp.at[slot], ag_r.at[slot], fsdp=mate)

    @pl.when(q + 1 < nq)
    def _():
        ag_up(f, gained).start()

    @pl.when(q > 0)
    def _():
        ag_down(f, gained).start()

    ag_mate(f, gained).start()

    def dp_copy(which, src, dst, k):
        return remote(src, dst.at[d], dp_s.at[which, k], dp_r.at[which, k], dp=(d + k) % ndp)

    for k in range(1, ndp):
        dp_copy(0, gained, dpx, k).start()
        dp_copy(1, grad, dpg, k).start()

    def ag_event(k):
        below, above = 2 * (q - k) + c, 2 * (q + k) + c

        @pl.when(q - k >= 0)
        def _():
            ag_up(below, ag.at[below]).wait_recv()

            @pl.when(q + 1 < nq)
            def _():
                ag_up(below, ag.at[below]).start()

            ag_mate(below, ag.at[below]).start()

        @pl.when(q + k < nq)
        def _():
            ag_down(above, ag.at[above]).wait_recv()

            @pl.when(q > 0)
            def _():
                ag_down(above, ag.at[above]).start()

            ag_mate(above, ag.at[above]).start()

    tenant = meta[0:1, :]
    owner = lax.broadcasted_iota(jnp.int32, (tenants * rank, rows), 0) // rank
    picked = owner.astype(F32) == tenant
    for at, lhs, rhs in ((0, down, gained), (rank, up, grad)):
        full = lax.dot_general(lhs[...], rhs[...], NT, preferred_element_type=F32)
        full = jnp.where(picked, full, 0.0).reshape(tenants, rank, rows)
        pk[at : at + rank, :] = jnp.sum(full, axis=0)
    pk[2 * rank : 2 * rank + 8, :] = meta[8:16, :]

    def pk_copy(k):
        return remote(pk, pkrx.at[k], pk_s.at[k], pk_r.at[k], fsdp=(f + k) % n)

    for k in range(1, n):
        pk_copy(k).start()
    ag[f] = gained[...]
    dpx[d] = gained[...]
    dpg[d] = grad[...]

    def chain_copy(t, rsem, rx, to):
        return remote(csend.at[t], rx.at[t], ch_s.at[t], rsem.at[t], fsdp=to)

    def chain_up(t):
        return chain_copy(t, up_r, uprx, (f + 2) % n)

    def chain_down(t):
        return chain_copy(t, dn_r, dnrx, (f + n - 2) % n)

    def mate_copy(t):
        return remote(psend.at[t], prx.at[t], pp_s.at[t], pp_r.at[t], fsdp=mate)

    def head(t):
        return ((t > q) & (q == 0)) | ((t < q) & (q == nq - 1))

    def chain(t):
        mate_copy(t).wait_recv()
        part[t] = (part[t].astype(F32) + prx[t].astype(F32)).astype(BF16)

        @pl.when((t > q) & (q > 0))
        def _():
            chain_up(t).wait_recv()
            csend[t] = (part[t].astype(F32) + uprx[t].astype(F32)).astype(BF16)

        @pl.when((t < q) & (q < nq - 1))
        def _():
            chain_down(t).wait_recv()
            csend[t] = (part[t].astype(F32) + dnrx[t].astype(F32)).astype(BF16)

        @pl.when(head(t))
        def _():
            csend[t] = part[t]

        @pl.when(t > q)
        def _():
            chain_up(t).start()

        @pl.when(t < q)
        def _():
            chain_down(t).start()

    def order(s):
        return xor(q, nq - 1 - s, nq)

    lag = min(2, nq - 1)
    period = -(-count // max(nq - 1, 1))
    in_back = min(count // period, nq - 1)

    @pl.loop(0, count)
    def _(i):
        load(i).wait()
        s, r = i // (2 * tpb), i % (2 * tpb)
        half, where = r // tpb, pl.ds(pl.multiple_of((r % tpb) * tile, tile), tile)
        t = order(s)
        out = lax.dot_general(
            wbuf[i % BUFFERS], grad[...], NT, preferred_element_type=F32
        ).astype(BF16)
        load(i + BUFFERS).start()

        @pl.when(half == 0)
        def _():
            psend[t, where, :] = out

        @pl.when(half == 1)
        def _():
            part[t, where, :] = out

        @pl.when(r == tpb - 1)
        def _():
            mate_copy(t).start()

        @pl.when((r == 2 * tpb - 1) & head(t))
        def _():
            chain(t)

        late = order(jnp.maximum(s - lag, 0))

        @pl.when((r == 2 * tpb - 1) & (s >= lag) & jnp.logical_not(head(late)))
        def _():
            chain(late)

        k = (i + 1) // period

        @pl.when(((i + 1) % period == 0) & (k < nq))
        def _():
            ag_event(k)

    total = pk[...]
    for k in range(1, n):
        pk_copy(k).wait_recv()
        total = total + pkrx[k]
    scale = lax.rsqrt(total[2 * rank : 2 * rank + 1, :] / width + RMS_EPS)
    inner = total[:rank, :] * scale
    back = total[rank : 2 * rank, :]
    sm[0:rank, :] = inner
    sm[rank : 2 * rank, :] = back * scale
    sm[2 * rank :, :] = jnp.concatenate([meta[1:2, :], total[2 * rank + 1 :, :]], axis=0)

    def sm_copy(k):
        return remote(sm, smrx.at[d], dp_s.at[2, k], dp_r.at[2, k], dp=(d + k) % ndp)

    for k in range(1, ndp):
        sm_copy(k).start()
    smrx[d] = sm[...]
    spread_a[...] = jnp.where(picked, jnp.tile(inner, (tenants, 1)), 0.0).astype(BF16)
    spread_b[...] = jnp.where(picked, jnp.tile(back, (tenants, 1)), 0.0).astype(BF16)
    scale_col[...] = jnp.broadcast_to(scale, (rows, rows)).T
    acc[...] = jnp.zeros_like(acc)

    @pl.loop(0, count)
    def _(i):
        s, r = i // (2 * tpb), i % (2 * tpb)
        half = r // tpb
        t = xor(q, s, nq)
        core = c * (1 - half) + (1 - c) * half
        slot = 2 * t + core

        @pl.when((r == 0) & (s + 1 < nq) & (s + 1 > in_back))
        def _():
            ag_event(s + 1)

        @pl.when(r == tpb)
        def _():
            ag_mate(slot, ag.at[slot]).wait_recv()

        load(count + i).wait()
        cols = pl.ds(pl.multiple_of((r % tpb) * tile, tile), tile)
        acc[...] += jnp.dot(
            ag[slot, :, cols], wbuf[(count + i) % BUFFERS], preferred_element_type=F32
        )

        @pl.when(i + BUFFERS < count)
        def _():
            load(count + i + BUFFERS).start()

        first = max(nq - lag, 0)
        for e in range(first, nq - 1):
            late = order(jnp.int32(e))

            @pl.when((i == (e - first + 1) * count // (nq - first) - 1) & jnp.logical_not(head(late)))
            def _():
                chain(late)

    for k in range(1, ndp):
        dp_copy(0, gained, dpx, k).wait_recv()
        dp_copy(1, grad, dpg, k).wait_recv()
        sm_copy(k).wait_recv()
    place = lax.broadcasted_iota(jnp.int32, (owned * rank, rows), 0) // rank + d * owned
    place = place.astype(F32)
    for at, src, dst, summed, base in ((rank, dpx, ga, sum_a, 0), (0, dpg, gb, sum_b, owned * rank)):
        lhs = jnp.concatenate(
            [
                jnp.where(
                    place == smrx[g, 2 * rank : 2 * rank + 1, :],
                    jnp.tile(smrx[g, at : at + rank, :], (owned, 1)),
                    0.0,
                ).astype(BF16)
                for g in range(ndp)
            ],
            axis=1,
        )
        step = min(512, local)
        for lo in range(0, local, step):
            rhs = src[:, :, lo : lo + step].reshape(ndp * rows, step)
            full = ADAPTER_SCALE * jnp.dot(lhs, rhs, preferred_element_type=F32)
            full = full.reshape(owned, rank, step)
            dst[:, :, lo : lo + step] = full
            sq = full * full + SQ_EPS
            summed[:, lo : lo + step] = jnp.sum(sq, axis=1)
            flat = sq.reshape(owned * rank, step)
            total = flat[:, 0:128]
            for w in range(128, step, 128):
                total = total + flat[:, w : w + 128]
            here = slice(base, base + owned * rank)
            if lo == 0:
                lanes[here, :] = total
            else:
                lanes[here, :] += total
    turned = lanes[...].T
    st[...] = jnp.sum(turned.reshape(16, 8, 2 * owned * rank), axis=0)

    def st_copy(k):
        return remote(st, strx.at[k], st_s.at[k], st_r.at[k], fsdp=(f + k) % n)

    for k in range(1, n):
        st_copy(k).start()

    chunk = min(512, local)
    for lo in range(0, local, chunk):
        cols = slice(lo, lo + chunk)
        adapted = lax.dot_general(spread_a[...], up[:, cols], TN, preferred_element_type=F32)
        wide = jnp.concatenate([scale_col[...]] * (chunk // rows), axis=1)
        projected[:, cols] = (acc[:, cols] * wide + ADAPTER_SCALE * adapted).astype(BF16)
    mate_copy(q).wait_recv()

    @pl.when(q > 0)
    def _():
        chain_up(q).wait_recv()

    @pl.when(q < nq - 1)
    def _():
        chain_down(q).wait_recv()

    for lo in range(0, local, chunk):
        here = slice(lo, lo + chunk)
        out = lax.dot_general(down[:, here], spread_b[...], TN, preferred_element_type=F32)
        out = ADAPTER_SCALE * out + part[q, here, :].astype(F32) + prx[q, here, :].astype(F32)
        lanes_up = jnp.where(q > 0, uprx[q, here, :].astype(F32), 0.0)
        lanes_dn = jnp.where(q < nq - 1, dnrx[q, here, :].astype(F32), 0.0)
        grad_t[here, :] = (out + lanes_up + lanes_dn).astype(BF16)

    whole = st[...]
    for k in range(1, n):
        st_copy(k).wait_recv()
        whole = whole + strx[k]
    stats[:, : 2 * owned * rank] = whole
    stats[:, 2 * owned * rank :] = sm[2 * rank :, :]

    for k in range(1, n):
        pk_copy(k).wait_send()
        st_copy(k).wait_send()
    for k in range(1, ndp):
        dp_copy(0, gained, dpx, k).wait_send()
        dp_copy(1, grad, dpg, k).wait_send()
        sm_copy(k).wait_send()

    @pl.loop(0, nq)
    def _(t):
        mate_copy(t).wait_send()
        slot = 2 * t + c

        @pl.when(t != q)
        def _():
            chain_up(t).wait_send()

        ag_mate(slot, ag.at[slot]).wait_send()

        @pl.when((t <= q) & (q + 1 < nq))
        def _():
            ag_up(slot, ag.at[slot]).wait_send()

        @pl.when((t >= q) & (q > 0))
        def _():
            ag_down(slot, ag.at[slot]).wait_send()


def on_device(
    ndp,
    n,
    inputs,
    norm_gain_vector,
    weight,
    down_adapters,
    up_adapters,
    tenant,
    tenant_slot_index,
    live_row_count,
    cotangent,
    down_row_factor,
    down_column_factor,
    up_row_factor,
    up_column_factor,
):
    rows, local = inputs.shape
    width = weight.shape[0]
    tenants, rank = down_adapters.shape[1:]
    owned = down_row_factor.shape[0]
    xf = inputs.astype(F32)
    gained = (xf * norm_gain_vector.astype(F32)).astype(BF16)
    live = lax.iota(jnp.int32, rows) < live_row_count[0]
    grad = jnp.where(live[:, None], cotangent, jnp.zeros_like(cotangent))
    pick = tenant[None, :] == lax.iota(jnp.int32, tenants)[:, None]
    slot = jnp.sum(jnp.where(pick, tenant_slot_index[:, None], 0), axis=0).astype(F32)
    power = jnp.sum(xf * xf, axis=1)
    factor_sum = jnp.pad(jnp.sum(down_row_factor, axis=1), (0, rows - owned))
    zero = jnp.zeros((6, rows), F32)
    meta = jnp.concatenate(
        [tenant.astype(F32)[None], slot[None], zero, power[None], factor_sum[None], zero], axis=0
    )
    down = jnp.transpose(down_adapters, (1, 2, 0)).reshape(tenants * rank, local)
    up = up_adapters.reshape(tenants * rank, local)
    tile = min(1024, local)
    nq = n // 2
    pieces = 2 * rank + 8
    cols = 2 * owned * rank
    vmem = pl.BlockSpec(memory_space=pltpu.VMEM)
    dma = pltpu.SemaphoreType.DMA
    half = pltpu.VMEM((nq, local, rows), BF16)
    projected, grad_t, ga, gb, sum_a, sum_b, stats = pl.pallas_call(
        functools.partial(kernel, ndp, n, rank, tenants, owned, width),
        out_shape=(
            jax.ShapeDtypeStruct((rows, local), BF16),
            jax.ShapeDtypeStruct((local, rows), BF16),
            jax.ShapeDtypeStruct((owned, rank, local), F32),
            jax.ShapeDtypeStruct((owned, rank, local), F32),
            jax.ShapeDtypeStruct((owned, local), F32),
            jax.ShapeDtypeStruct((owned, local), F32),
            jax.ShapeDtypeStruct((8, cols + rows), F32),
        ),
        in_specs=[vmem] * 5 + [pl.BlockSpec(memory_space=pl.ANY)],
        out_specs=(vmem,) * 7,
        scratch_shapes=[
            pltpu.VMEM((BUFFERS, tile, local), BF16),
            pltpu.VMEM((n, rows, local), BF16),
            pltpu.VMEM((ndp, rows, local), BF16),
            pltpu.VMEM((ndp, rows, local), BF16),
            pltpu.VMEM((rows, local), F32),
            half, half, half, half, half, half,
            pltpu.VMEM((pieces, rows), F32),
            pltpu.VMEM((n, pieces, rows), F32),
            pltpu.VMEM((pieces, rows), F32),
            pltpu.VMEM((ndp, pieces, rows), F32),
            pltpu.VMEM((8, cols), F32),
            pltpu.VMEM((n, 8, cols), F32),
            pltpu.VMEM((tenants * rank, rows), BF16),
            pltpu.VMEM((tenants * rank, rows), BF16),
            pltpu.VMEM((cols, 128), F32),
            pltpu.VMEM((rows, rows), F32),
            dma((BUFFERS,)),
            dma((n, 2)),
            dma((n,)),
            dma((n,)),
            dma((3, ndp)),
            dma((3, ndp)),
            dma((nq,)),
            dma((nq,)),
            dma((nq,)),
            dma((nq,)),
            dma((nq,)),
            dma((n,)),
            dma((n,)),
            dma((n,)),
            dma((n,)),
        ],
        compiler_params=pltpu.CompilerParams(
            collective_id=0, has_side_effects=True, vmem_limit_bytes=60 * 1024 * 1024
        ),
    )(gained, grad, meta, down, up, weight)

    row_a_new = BETA_TWO * down_row_factor + (1.0 - BETA_TWO) * (sum_a / rank)
    col_b_new = BETA_TWO * up_column_factor + (1.0 - BETA_TWO) * (sum_b / rank)
    sums = jnp.sum(stats[:, :cols], axis=0).reshape(2, owned, rank)
    col_a_new = BETA_TWO * down_column_factor + (1.0 - BETA_TWO) * (sums[0] / width)
    row_b_new = BETA_TWO * up_row_factor + (1.0 - BETA_TWO) * (sums[1] / width)
    kept = stats[1, cols : cols + owned]
    mean_a = (BETA_TWO * kept + (1.0 - BETA_TWO) * (jnp.sum(sums[0], axis=1) / rank)) / width
    mean_b = jnp.sum(row_b_new, axis=1) / rank
    update_a = ga * lax.rsqrt(row_a_new[:, None, :] * col_a_new[:, :, None] / mean_a[:, None, None])
    update_b = gb * lax.rsqrt(row_b_new[:, :, None] * col_b_new[:, None, :] / mean_b[:, None, None])
    return (
        projected,
        grad_t,
        jnp.swapaxes(update_a, 1, 2),
        update_b,
        row_a_new,
        col_a_new,
        row_b_new,
        col_b_new,
    )


def solution(mesh):
    return jax.shard_map(
        functools.partial(on_device, mesh.shape["dp"], mesh.shape["fsdp"]),
        mesh=mesh,
        in_specs=(
            P("dp", "fsdp"),
            P("fsdp"),
            P(None, "fsdp"),
            P("fsdp", None, None),
            P(None, None, "fsdp"),
            P("dp"),
            P(),
            P("dp"),
            P("dp", "fsdp"),
            P("dp", "fsdp"),
            P("dp", None),
            P("dp", None),
            P("dp", "fsdp"),
        ),
        out_specs=(
            P("dp", "fsdp"),
            P("fsdp", "dp"),
            P("dp", "fsdp", None),
            P("dp", None, "fsdp"),
            P("dp", "fsdp"),
            P("dp", None),
            P("dp", None),
            P("dp", "fsdp"),
        ),
        check_vma=False,
    )
```

```python
import functools

import jax
import jax.numpy as jnp
from jax import lax
from jax.experimental import pallas as pl
from jax.experimental.pallas import tpu as pltpu
from jax.sharding import PartitionSpec as P

ADAPTER_SCALE = 0.5
BETA_TWO = 0.9
SQ_EPS = 1e-30
RMS_EPS = 1e-05
BUFFERS = 3
NT = (((1,), (1,)), ((), ()))
TN = (((0,), (0,)), ((), ()))
F32, BF16 = jnp.float32, jnp.bfloat16
MESH = pl.DeviceIdType.MESH


def xor(a, b, count):
    out, bit = 0, 1
    while bit < count:
        out = out + ((a // bit + b // bit) % 2) * bit
        bit *= 2
    return out


def kernel(
    ndp, n, rank, tenants, owned, width,
    gained, grad, meta, down, up, weight,
    projected, grad_t, ga, gb, sum_a, sum_b, stats,
    wbuf, ag, dpx, dpg, acc, part, psend, prx, csend, uprx, dnrx,
    pk, pkrx, sm, smrx, st, strx, spread_a, spread_b, lanes, scale_col,
    wsem, ag_s, ag_sp, ag_r, dp_s, dp_r, pp_s, pp_r, ch_s, up_r, dn_r, pk_s, pk_r, st_s, st_r,
):
    rows, local = gained.shape
    tile = wbuf.shape[1]
    tpb = local // tile
    nq = n // 2
    count = 2 * nq * tpb
    d = lax.axis_index("dp")
    f = lax.axis_index("fsdp")
    q, c = f // 2, f % 2
    mate = 2 * q + 1 - c

    def remote(src, dst, ssem, rsem, **where):
        return pltpu.make_async_remote_copy(
            src_ref=src, dst_ref=dst, send_sem=ssem, recv_sem=rsem,
            device_id=where, device_id_type=MESH,
        )

    def order(s):
        low = q < nq // 2
        at = jnp.where(low, q, nq - 1 - q)
        t = jnp.where(s < nq - 1 - at, nq - 1 - s, s - (nq - 1 - at))
        return jnp.where(low, t, nq - 1 - t)

    def start_row(i):
        i2 = i % count
        back = i // count == 0
        s, r = i2 // (2 * tpb), i2 % (2 * tpb)
        half = r // tpb
        t = jnp.where(back, order(s), xor(q, s, nq))
        core = jnp.where(back, (1 - c) * (1 - half) + c * half, c * (1 - half) + (1 - c) * half)
        return (2 * t + core) * local + (r % tpb) * tile

    def load(i):
        return pltpu.make_async_copy(
            weight.at[pl.ds(pl.multiple_of(start_row(i), tile), tile), :],
            wbuf.at[i % BUFFERS], wsem.at[i % BUFFERS],
        )

    for i in range(BUFFERS):
        load(jnp.int32(i)).start()

    barrier = pltpu.get_barrier_semaphore()
    for k in range(1, n):
        pl.semaphore_signal(barrier, inc=1, device_id={"fsdp": (f + k) % n}, device_id_type=MESH)
    for k in range(1, ndp):
        pl.semaphore_signal(barrier, inc=1, device_id={"dp": (d + k) % ndp}, device_id_type=MESH)
    pl.semaphore_wait(barrier, n - 1 + ndp - 1)

    def ag_up(slot, src):
        return remote(src, ag.at[slot], ag_s.at[slot, 0], ag_r.at[slot], fsdp=(f + 2) % n)

    def ag_down(slot, src):
        return remote(src, ag.at[slot], ag_s.at[slot, 1], ag_r.at[slot], fsdp=(f + n - 2) % n)

    def ag_mate(slot, src):
        return remote(src, ag.at[slot], ag_sp.at[slot], ag_r.at[slot], fsdp=mate)

    @pl.when(q + 1 < nq)
    def _():
        ag_up(f, gained).start()

    @pl.when(q > 0)
    def _():
        ag_down(f, gained).start()

    ag_mate(f, gained).start()

    def dp_copy(which, src, dst, k):
        return remote(src, dst.at[d], dp_s.at[which, k], dp_r.at[which, k], dp=(d + k) % ndp)

    for k in range(1, ndp):
        dp_copy(0, gained, dpx, k).start()
        dp_copy(1, grad, dpg, k).start()

    def ag_event(k):
        below, above = 2 * (q - k) + c, 2 * (q + k) + c

        @pl.when(q - k >= 0)
        def _():
            ag_up(below, ag.at[below]).wait_recv()

            @pl.when(q + 1 < nq)
            def _():
                ag_up(below, ag.at[below]).start()

            ag_mate(below, ag.at[below]).start()

        @pl.when(q + k < nq)
        def _():
            ag_down(above, ag.at[above]).wait_recv()

            @pl.when(q > 0)
            def _():
                ag_down(above, ag.at[above]).start()

            ag_mate(above, ag.at[above]).start()

    tenant = meta[0:1, :]
    owner = lax.broadcasted_iota(jnp.int32, (tenants * rank, rows), 0) // rank
    picked = owner.astype(F32) == tenant
    for at, lhs, rhs in ((0, down, gained), (rank, up, grad)):
        full = lax.dot_general(lhs[...], rhs[...], NT, preferred_element_type=F32)
        full = jnp.where(picked, full, 0.0).reshape(tenants, rank, rows)
        pk[at : at + rank, :] = jnp.sum(full, axis=0)
    pk[2 * rank : 2 * rank + 8, :] = meta[8:16, :]

    def pk_copy(k):
        return remote(pk, pkrx.at[k], pk_s.at[k], pk_r.at[k], fsdp=(f + k) % n)

    for k in range(1, n):
        pk_copy(k).start()
    ag[f] = gained[...]
    dpx[d] = gained[...]
    dpg[d] = grad[...]

    def chain_copy(t, rsem, rx, to):
        return remote(csend.at[t], rx.at[t], ch_s.at[t], rsem.at[t], fsdp=to)

    def chain_up(t):
        return chain_copy(t, up_r, uprx, (f + 2) % n)

    def chain_down(t):
        return chain_copy(t, dn_r, dnrx, (f + n - 2) % n)

    def mate_copy(t):
        return remote(psend.at[t], prx.at[t], pp_s.at[t], pp_r.at[t], fsdp=mate)

    def head(t):
        return ((t > q) & (q == 0)) | ((t < q) & (q == nq - 1))

    def chain(t):
        mate_copy(t).wait_recv()
        part[t] = (part[t].astype(F32) + prx[t].astype(F32)).astype(BF16)

        @pl.when((t > q) & (q > 0))
        def _():
            chain_up(t).wait_recv()
            csend[t] = (part[t].astype(F32) + uprx[t].astype(F32)).astype(BF16)

        @pl.when((t < q) & (q < nq - 1))
        def _():
            chain_down(t).wait_recv()
            csend[t] = (part[t].astype(F32) + dnrx[t].astype(F32)).astype(BF16)

        @pl.when(head(t))
        def _():
            csend[t] = part[t]

        @pl.when(t > q)
        def _():
            chain_up(t).start()

        @pl.when(t < q)
        def _():
            chain_down(t).start()

    lag = min(2, nq - 1)
    period = max(count // max(nq - 1, 1), 1)
    in_back = max(min(count // period, nq - 2), 0)

    @pl.loop(0, count)
    def _(i):
        load(i).wait()
        s, r = i // (2 * tpb), i % (2 * tpb)
        half, where = r // tpb, pl.ds(pl.multiple_of((r % tpb) * tile, tile), tile)
        t = order(s)
        out = lax.dot_general(
            wbuf[i % BUFFERS], grad[...], NT, preferred_element_type=F32
        ).astype(BF16)
        load(i + BUFFERS).start()

        @pl.when(half == 0)
        def _():
            psend[t, where, :] = out

        @pl.when(half == 1)
        def _():
            part[t, where, :] = out

        @pl.when(r == tpb - 1)
        def _():
            mate_copy(t).start()

        @pl.when((r == 2 * tpb - 1) & head(t))
        def _():
            chain(t)

        late = order(jnp.maximum(s - lag, 0))

        @pl.when((r == 2 * tpb - 1) & (s >= lag) & jnp.logical_not(head(late)))
        def _():
            chain(late)

        k = (i + 1) // period

        @pl.when(((i + 1) % period == 0) & (k <= in_back))
        def _():
            ag_event(k)

    total = pk[...]
    for k in range(1, n):
        pk_copy(k).wait_recv()
        total = total + pkrx[k]
    scale = lax.rsqrt(total[2 * rank : 2 * rank + 1, :] / width + RMS_EPS)
    inner = total[:rank, :] * scale
    back = total[rank : 2 * rank, :]
    sm[0:rank, :] = inner
    sm[rank : 2 * rank, :] = back * scale
    sm[2 * rank :, :] = jnp.concatenate([meta[1:2, :], total[2 * rank + 1 :, :]], axis=0)

    def sm_copy(k):
        return remote(sm, smrx.at[d], dp_s.at[2, k], dp_r.at[2, k], dp=(d + k) % ndp)

    for k in range(1, ndp):
        sm_copy(k).start()
    smrx[d] = sm[...]
    spread_a[...] = jnp.where(picked, jnp.tile(inner, (tenants, 1)), 0.0).astype(BF16)
    spread_b[...] = jnp.where(picked, jnp.tile(back, (tenants, 1)), 0.0).astype(BF16)
    scale_col[...] = jnp.broadcast_to(scale, (rows, rows)).T
    acc[...] = jnp.zeros_like(acc)

    @pl.loop(0, count)
    def _(i):
        s, r = i // (2 * tpb), i % (2 * tpb)
        half = r // tpb
        t = xor(q, s, nq)
        core = c * (1 - half) + (1 - c) * half
        slot = 2 * t + core

        @pl.when((r == 0) & (s + 1 < nq) & (s + 1 > in_back))
        def _():
            ag_event(s + 1)

        @pl.when(r == tpb)
        def _():
            ag_mate(slot, ag.at[slot]).wait_recv()

        load(count + i).wait()
        cols = pl.ds(pl.multiple_of((r % tpb) * tile, tile), tile)
        acc[...] += jnp.dot(
            ag[slot, :, cols], wbuf[(count + i) % BUFFERS], preferred_element_type=F32
        )

        @pl.when(i + BUFFERS < count)
        def _():
            load(count + i + BUFFERS).start()

        first = max(nq - lag, 0)
        for e in range(first, nq - 1):
            late = order(jnp.int32(e))

            @pl.when((i == 2 * (e - first + 1)) & jnp.logical_not(head(late)))
            def _():
                chain(late)

    for k in range(1, ndp):
        dp_copy(0, gained, dpx, k).wait_recv()
        dp_copy(1, grad, dpg, k).wait_recv()
        sm_copy(k).wait_recv()
    place = lax.broadcasted_iota(jnp.int32, (owned * rank, rows), 0) // rank + d * owned
    place = place.astype(F32)
    for at, src, dst, summed, base in ((rank, dpx, ga, sum_a, 0), (0, dpg, gb, sum_b, owned * rank)):
        lhs = jnp.concatenate(
            [
                jnp.where(
                    place == smrx[g, 2 * rank : 2 * rank + 1, :],
                    jnp.tile(smrx[g, at : at + rank, :], (owned, 1)),
                    0.0,
                ).astype(BF16)
                for g in range(ndp)
            ],
            axis=1,
        )
        step = min(512, local)
        for lo in range(0, local, step):
            rhs = src[:, :, lo : lo + step].reshape(ndp * rows, step)
            full = ADAPTER_SCALE * jnp.dot(lhs, rhs, preferred_element_type=F32)
            full = full.reshape(owned, rank, step)
            dst[:, :, lo : lo + step] = full
            sq = full * full + SQ_EPS
            summed[:, lo : lo + step] = jnp.sum(sq, axis=1)
            flat = sq.reshape(owned * rank, step)
            total = flat[:, 0:128]
            for w in range(128, step, 128):
                total = total + flat[:, w : w + 128]
            here = slice(base, base + owned * rank)
            if lo == 0:
                lanes[here, :] = total
            else:
                lanes[here, :] += total
    turned = lanes[...].T
    st[...] = jnp.sum(turned.reshape(16, 8, 2 * owned * rank), axis=0)

    def st_copy(k):
        return remote(st, strx.at[k], st_s.at[k], st_r.at[k], fsdp=(f + k) % n)

    for k in range(1, n):
        st_copy(k).start()

    chunk = min(512, local)
    for lo in range(0, local, chunk):
        cols = slice(lo, lo + chunk)
        adapted = lax.dot_general(spread_a[...], up[:, cols], TN, preferred_element_type=F32)
        wide = jnp.concatenate([scale_col[...]] * (chunk // rows), axis=1)
        projected[:, cols] = (acc[:, cols] * wide + ADAPTER_SCALE * adapted).astype(BF16)
    mate_copy(q).wait_recv()

    @pl.when(q > 0)
    def _():
        chain_up(q).wait_recv()

    @pl.when(q < nq - 1)
    def _():
        chain_down(q).wait_recv()

    for lo in range(0, local, chunk):
        here = slice(lo, lo + chunk)
        out = lax.dot_general(down[:, here], spread_b[...], TN, preferred_element_type=F32)
        out = ADAPTER_SCALE * out + part[q, here, :].astype(F32) + prx[q, here, :].astype(F32)
        lanes_up = jnp.where(q > 0, uprx[q, here, :].astype(F32), 0.0)
        lanes_dn = jnp.where(q < nq - 1, dnrx[q, here, :].astype(F32), 0.0)
        grad_t[here, :] = (out + lanes_up + lanes_dn).astype(BF16)

    whole = st[...]
    for k in range(1, n):
        st_copy(k).wait_recv()
        whole = whole + strx[k]
    stats[:, : 2 * owned * rank] = whole
    stats[:, 2 * owned * rank :] = sm[2 * rank :, :]

    for k in range(1, n):
        pk_copy(k).wait_send()
        st_copy(k).wait_send()
    for k in range(1, ndp):
        dp_copy(0, gained, dpx, k).wait_send()
        dp_copy(1, grad, dpg, k).wait_send()
        sm_copy(k).wait_send()

    @pl.loop(0, nq)
    def _(t):
        mate_copy(t).wait_send()
        slot = 2 * t + c

        @pl.when(t != q)
        def _():
            chain_up(t).wait_send()

        ag_mate(slot, ag.at[slot]).wait_send()

        @pl.when((t <= q) & (q + 1 < nq))
        def _():
            ag_up(slot, ag.at[slot]).wait_send()

        @pl.when((t >= q) & (q > 0))
        def _():
            ag_down(slot, ag.at[slot]).wait_send()


def on_device(
    ndp,
    n,
    inputs,
    norm_gain_vector,
    weight,
    down_adapters,
    up_adapters,
    tenant,
    tenant_slot_index,
    live_row_count,
    cotangent,
    down_row_factor,
    down_column_factor,
    up_row_factor,
    up_column_factor,
):
    rows, local = inputs.shape
    width = weight.shape[0]
    tenants, rank = down_adapters.shape[1:]
    owned = down_row_factor.shape[0]
    xf = inputs.astype(F32)
    gained = (xf * norm_gain_vector.astype(F32)).astype(BF16)
    live = lax.iota(jnp.int32, rows) < live_row_count[0]
    grad = jnp.where(live[:, None], cotangent, jnp.zeros_like(cotangent))
    pick = tenant[None, :] == lax.iota(jnp.int32, tenants)[:, None]
    slot = jnp.sum(jnp.where(pick, tenant_slot_index[:, None], 0), axis=0).astype(F32)
    power = jnp.sum(xf * xf, axis=1)
    factor_sum = jnp.pad(jnp.sum(down_row_factor, axis=1), (0, rows - owned))
    zero = jnp.zeros((6, rows), F32)
    meta = jnp.concatenate(
        [tenant.astype(F32)[None], slot[None], zero, power[None], factor_sum[None], zero], axis=0
    )
    down = jnp.transpose(down_adapters, (1, 2, 0)).reshape(tenants * rank, local)
    up = up_adapters.reshape(tenants * rank, local)
    tile = min(1024, local)
    nq = n // 2
    pieces = 2 * rank + 8
    cols = 2 * owned * rank
    vmem = pl.BlockSpec(memory_space=pltpu.VMEM)
    dma = pltpu.SemaphoreType.DMA
    half = pltpu.VMEM((nq, local, rows), BF16)
    projected, grad_t, ga, gb, sum_a, sum_b, stats = pl.pallas_call(
        functools.partial(kernel, ndp, n, rank, tenants, owned, width),
        out_shape=(
            jax.ShapeDtypeStruct((rows, local), BF16),
            jax.ShapeDtypeStruct((local, rows), BF16),
            jax.ShapeDtypeStruct((owned, rank, local), F32),
            jax.ShapeDtypeStruct((owned, rank, local), F32),
            jax.ShapeDtypeStruct((owned, local), F32),
            jax.ShapeDtypeStruct((owned, local), F32),
            jax.ShapeDtypeStruct((8, cols + rows), F32),
        ),
        in_specs=[vmem] * 5 + [pl.BlockSpec(memory_space=pl.ANY)],
        out_specs=(vmem,) * 7,
        scratch_shapes=[
            pltpu.VMEM((BUFFERS, tile, local), BF16),
            pltpu.VMEM((n, rows, local), BF16),
            pltpu.VMEM((ndp, rows, local), BF16),
            pltpu.VMEM((ndp, rows, local), BF16),
            pltpu.VMEM((rows, local), F32),
            half, half, half, half, half, half,
            pltpu.VMEM((pieces, rows), F32),
            pltpu.VMEM((n, pieces, rows), F32),
            pltpu.VMEM((pieces, rows), F32),
            pltpu.VMEM((ndp, pieces, rows), F32),
            pltpu.VMEM((8, cols), F32),
            pltpu.VMEM((n, 8, cols), F32),
            pltpu.VMEM((tenants * rank, rows), BF16),
            pltpu.VMEM((tenants * rank, rows), BF16),
            pltpu.VMEM((cols, 128), F32),
            pltpu.VMEM((rows, rows), F32),
            dma((BUFFERS,)),
            dma((n, 2)),
            dma((n,)),
            dma((n,)),
            dma((3, ndp)),
            dma((3, ndp)),
            dma((nq,)),
            dma((nq,)),
            dma((nq,)),
            dma((nq,)),
            dma((nq,)),
            dma((n,)),
            dma((n,)),
            dma((n,)),
            dma((n,)),
        ],
        compiler_params=pltpu.CompilerParams(
            collective_id=0, has_side_effects=True, vmem_limit_bytes=60 * 1024 * 1024
        ),
    )(gained, grad, meta, down, up, weight)

    row_a_new = BETA_TWO * down_row_factor + (1.0 - BETA_TWO) * (sum_a / rank)
    col_b_new = BETA_TWO * up_column_factor + (1.0 - BETA_TWO) * (sum_b / rank)
    sums = jnp.sum(stats[:, :cols], axis=0).reshape(2, owned, rank)
    col_a_new = BETA_TWO * down_column_factor + (1.0 - BETA_TWO) * (sums[0] / width)
    row_b_new = BETA_TWO * up_row_factor + (1.0 - BETA_TWO) * (sums[1] / width)
    kept = stats[1, cols : cols + owned]
    mean_a = (BETA_TWO * kept + (1.0 - BETA_TWO) * (jnp.sum(sums[0], axis=1) / rank)) / width
    mean_b = jnp.sum(row_b_new, axis=1) / rank
    update_a = ga * lax.rsqrt(row_a_new[:, None, :] * col_a_new[:, :, None] / mean_a[:, None, None])
    update_b = gb * lax.rsqrt(row_b_new[:, :, None] * col_b_new[:, None, :] / mean_b[:, None, None])
    return (
        projected,
        grad_t,
        jnp.swapaxes(update_a, 1, 2),
        update_b,
        row_a_new,
        col_a_new,
        row_b_new,
        col_b_new,
    )


def solution(mesh):
    return jax.shard_map(
        functools.partial(on_device, mesh.shape["dp"], mesh.shape["fsdp"]),
        mesh=mesh,
        in_specs=(
            P("dp", "fsdp"),
            P("fsdp"),
            P(None, "fsdp"),
            P("fsdp", None, None),
            P(None, None, "fsdp"),
            P("dp"),
            P(),
            P("dp"),
            P("dp", "fsdp"),
            P("dp", "fsdp"),
            P("dp", None),
            P("dp", None),
            P("dp", "fsdp"),
        ),
        out_specs=(
            P("dp", "fsdp"),
            P("fsdp", "dp"),
            P("dp", "fsdp", None),
            P("dp", None, "fsdp"),
            P("dp", "fsdp"),
            P("dp", None),
            P("dp", None),
            P("dp", "fsdp"),
        ),
        check_vma=False,
    )
```
